256 devices in a mesh: ctx: 32 (over x_hi, z, core), ch: 8 (over y, x_lo).
Axes of the slice: x: 4 (x_hi: 2, x_lo: 2; x = x_hi * 2 + x_lo), y: 4, z: 8, core: 2. Of those that a mesh axis runs over, the one named last changes fastest.
Arguments:
- saved_input: bfloat16 [32, 16, 98304], P(None, 'ch', 'ctx'), may hold values from -6 to 6
- out_grad: bfloat16 [32, 16, 98304], P(None, 'ch', 'ctx'), may hold values from -6 to 6
- block_offsets: int32 [16], replicated, may hold values from 1 to 743, as said below
- head_len: int32 [1], replicated, may hold values from 16 to 128
Outputs:
- grad_filter: float32 [32, 2176], P(None, 'ctx')
The draws below stay inside these ranges and needn't reach their ends.
Inputs may be any that keep to these rules, and one draw needn't show every extreme that they name: `block_offsets`: 16 distinct values; the largest is 743.
All inputs are finite; a program needn't handle non-finite values.
Results may differ from the reference program's by a relative error of at most 0.0003.
Values may be sent and summed in bfloat16 or wider, within the bound.
No kernel may reach another device: no remote copies, remote signals or barrier semaphores. Data moves between devices by JAX's collectives and lax.ppermute only.
A program may use at most 64 MiB of HBM per device.

```python
import math
import jax
import jax.numpy as jnp
from jax import lax

GSIZE = 16
FILT = 32
NBLK = 16
TOKENS = 98304
LAGTILES = 744


def draw_block_offsets(key, part):
    first_key, second_key = jax.random.split(jax.random.fold_in(key, 11))
    picked = jax.random.permutation(first_key, LAGTILES - 2)[:NBLK - 1] + 1
    listed = jnp.concatenate([picked, jnp.full((1,), LAGTILES - 1)]).astype(jnp.int32)
    return jax.random.permutation(second_key, listed)


def steps_of(own_key, shape, cuts, least, top_value):
    loudness, own = 1.0, jax.random.fold_in(own_key, 6)
    for position, shards_of in cuts:
        heights = jnp.exp(jax.random.uniform(jax.random.fold_in(own, position), (shards_of,), jnp.float32, least / len(cuts), top_value / len(cuts)))
        loudness = loudness * jnp.repeat(heights, shape[position] // shards_of).reshape([-1 if axis == position else 1 for axis in range(len(shape))])
    return loudness


def noise(rng, dims, scale, most, shards=(), kind=jnp.bfloat16):
    values = scale * jax.random.normal(rng, dims, jnp.float32)
    if shards:
        values = values * steps_of(rng, dims, shards, -0.22, 0.18)
    return jnp.clip(values, -most, most).astype(kind)


def setup_inputs(seed: int = 0) -> dict:
    keys = jax.random.split(jax.random.key(seed), 5)
    saved_input = noise(keys[0], (FILT, GSIZE, TOKENS), 1.0, 6.0, ((1, 8), (2, 32)))
    out_grad = noise(keys[1], (FILT, GSIZE, TOKENS), 1.0, 6.0, ((1, 8), (2, 32)))
    block_offsets = draw_block_offsets(jax.random.fold_in(keys[4], 71), 0)
    head_len = jax.random.randint(keys[3], (1,), 16, 129).astype(jnp.int32)
    return dict(saved_input=saved_input, out_grad=out_grad, block_offsets=block_offsets, head_len=head_len)


def diagonals(lag_grid):
    flipped = lag_grid[:, ::-1]
    diag_band = flipped.reshape(-1)[127:127 + 255 * 128].reshape(128, 255)[:, :128]
    return lax.optimization_barrier(jnp.sum(diag_band, axis=0))

def reference(saved_input, out_grad, block_offsets, head_len):
    tile_count = TOKENS // 128
    pad_width = (LAGTILES + 1) * 128
    offsets = jnp.concatenate([jnp.zeros((1,), jnp.int32), block_offsets.astype(jnp.int32)])

    def per_filter(filter_item):
        input_rows, grad_part = filter_item
        padded_x = jnp.concatenate([jnp.zeros((GSIZE, pad_width), jnp.float32), input_rows.astype(jnp.float32)], axis=1)
        grad_rows = grad_part.astype(jnp.float32).reshape(GSIZE, tile_count, 128)

        def per_block(offset):
            slice_start = (pad_width - (offset + 1) * 128).astype(jnp.int32)
            window_span = lax.dynamic_slice_in_dim(padded_x, slice_start, (tile_count + 1) * 128, 1)
            left_tiles = window_span[:, :tile_count * 128].reshape(GSIZE, tile_count, 128)
            right_tiles = window_span[:, 128:].reshape(GSIZE, tile_count, 128)
            window = jnp.concatenate([left_tiles, right_tiles], axis=2)
            lag_grid = jnp.einsum('gai,gak->ik', grad_rows, window, precision=lax.Precision.HIGHEST)
            return diagonals(lag_grid)
        return lax.map(per_block, offsets).reshape(-1)
    lag_sums = lax.map(per_filter, (saved_input, out_grad))
    lag_index = lax.broadcasted_iota(jnp.int32, (1, (NBLK + 1) * 128), 1)
    keep_mask = (lag_index >= 128) | (lag_index < head_len[0])
    loss_scale = 1.0 / math.sqrt(TOKENS * GSIZE)
    return jnp.where(keep_mask, lag_sums, jnp.zeros_like(lag_sums)) * loss_scale
```

```python
import math

import jax
import jax.numpy as jnp
from jax import lax
from jax.experimental import pallas as pl
from jax.experimental.pallas import tpu as pltpu
from jax.sharding import PartitionSpec as P

LANES = 128


def lag_kernel(scale, offsets_ref, head_ref, both_ref, out_ref, x_ref, y_ref, xt_ref, diag_ref, sems):
    shards, pair_tiles = both_ref.shape[:2]
    per = pair_tiles // 2
    tiles = shards * per
    rows = 2 * tiles
    def shard_view(ref, first):
        return ref.at[pl.ds(first, tiles)].reshape(shards, per, 2, LANES)

    copies = [
        pltpu.make_async_copy(both_ref.at[:, pl.ds(0, per)], shard_view(x_ref, 1), sems.at[0]),
        pltpu.make_async_copy(both_ref.at[:, pl.ds(per, per)], shard_view(y_ref, 0), sems.at[1]),
    ]
    for c in copies:
        c.start()
    x_ref[0] = jnp.zeros((2, LANES), x_ref.dtype)
    y_tail = y_ref.at[pl.ds(tiles, tiles)].reshape(rows, LANES)
    y_tail[...] = jnp.zeros((rows, LANES), y_ref.dtype)
    for c in copies:
        c.wait()
    for part, first in ((0, 1), (1, 0)):
        xs = x_ref.at[pl.ds(first, tiles)].reshape(rows, LANES)
        xt_ref[pl.ds(part * LANES, LANES), :] = xs[...].T
    blocks = out_ref.shape[0]
    keep = lax.broadcasted_iota(jnp.int32, (LANES, LANES), 0) <= lax.broadcasted_iota(
        jnp.int32, (LANES, LANES), 1)
    xt = xt_ref[...]
    for k in range(0, blocks, 2):
        group = [j for j in (k, k + 1) if j < blocks]
        windows = []
        for j in group:
            start = 0 if j == 0 else offsets_ref[j - 1]
            windows.append(y_ref.at[pl.ds(start, tiles)].reshape(rows, LANES)[...])
        window = jnp.concatenate(windows, axis=1) if len(windows) > 1 else windows[0]
        grid = jnp.dot(xt, window, preferred_element_type=jnp.float32)
        for n, j in enumerate(group):
            part = grid[:, n * LANES:(n + 1) * LANES]
            both = jnp.where(keep, part[:LANES], part[LANES:])
            acc = both[:8]
            for v in range(1, LANES // 8):
                acc = acc + pltpu.roll(both[8 * v:8 * v + 8], LANES - 8 * v, 1)
            diag_ref[pl.ds(8 * j, 8), :] = acc
    acc = diag_ref[...]
    sub = lax.broadcasted_iota(jnp.int32, acc.shape, 0)
    for bit in (1, 2, 4):
        acc = jnp.where((sub & bit) != 0, pltpu.roll(acc, LANES - bit, 1), acc)
    sums = jnp.sum(acc.reshape(blocks, 8, LANES), axis=1) * scale
    block = lax.broadcasted_iota(jnp.int32, sums.shape, 0)
    lag = lax.broadcasted_iota(jnp.int32, sums.shape, 1)
    out_ref[...] = jnp.where((block > 0) | (lag < head_ref[0]), sums, jnp.zeros_like(sums))


def lag_sums(both, offsets, head_len, scale):
    shards, pair_tiles = both.shape[:2]
    tiles = shards * pair_tiles // 2
    blocks = offsets.shape[0] + 1
    return pl.pallas_call(
        lambda *refs: lag_kernel(scale, *refs),
        out_shape=jax.ShapeDtypeStruct((blocks, LANES), jnp.float32),
        in_specs=[
            pl.BlockSpec(memory_space=pltpu.SMEM),
            pl.BlockSpec(memory_space=pltpu.SMEM),
            pl.BlockSpec(memory_space=pl.ANY),
        ],
        out_specs=pl.BlockSpec(memory_space=pltpu.VMEM),
        scratch_shapes=[
            pltpu.VMEM((tiles + 1, 2, LANES), both.dtype),
            pltpu.VMEM((2 * tiles, 2, LANES), both.dtype),
            pltpu.VMEM((2 * LANES, 2 * tiles), both.dtype),
            pltpu.VMEM((8 * blocks, LANES), jnp.float32),
            pltpu.SemaphoreType.DMA((2,)),
        ],
    )(offsets, head_len, both)


def local(saved_input, out_grad, block_offsets, head_len):
    filters, local_ch, tok_dev = saved_input.shape
    ctx_count, ch_count = lax.axis_size("ctx"), lax.axis_size("ch")
    scale = 1.0 / math.sqrt(tok_dev * ctx_count * local_ch * ch_count)
    both = jnp.concatenate([saved_input, out_grad], axis=2)
    both = lax.all_to_all(both, "ctx", split_axis=0, concat_axis=0, tiled=True)
    tiles = both.shape[2] // LANES
    both = both.reshape(ctx_count, local_ch, tiles, LANES).transpose(0, 2, 1, 3)
    sums = lag_sums(both, block_offsets, head_len, scale)
    pieces = sums.reshape(ctx_count, 1, -1)
    pieces = jnp.broadcast_to(pieces, (ctx_count, ch_count, pieces.shape[2]))
    pieces = pieces.reshape(ctx_count * ch_count, -1)
    got = lax.all_to_all(pieces, ("ctx", "ch"), split_axis=0, concat_axis=0, tiled=True)
    return jnp.sum(got.reshape(filters, ch_count, -1), axis=1)


def solution(mesh):
    in_specs = (P(None, "ch", "ctx"), P(None, "ch", "ctx"), P(), P())
    return jax.shard_map(
        local, mesh=mesh, in_specs=in_specs, out_specs=P(None, "ctx"), check_vma=False
    )
```

```python
import functools
import math

import jax
import jax.numpy as jnp
from jax import lax
from jax.experimental import pallas as pl
from jax.experimental.pallas import tpu as pltpu
from jax.sharding import PartitionSpec as P

LANES = 128
VMEM = pl.BlockSpec(memory_space=pltpu.VMEM)
SMEM = pl.BlockSpec(memory_space=pltpu.SMEM)
ANY = pl.BlockSpec(memory_space=pl.ANY)


def join_kernel(a_ref, b_ref, out_ref, sems):
    width = a_ref.shape[2]
    copies = [
        pltpu.make_async_copy(a_ref, out_ref.at[:, :, pl.ds(0, width)], sems.at[0]),
        pltpu.make_async_copy(b_ref, out_ref.at[:, :, pl.ds(width, width)], sems.at[1]),
    ]
    for c in copies:
        c.start()
    for c in copies:
        c.wait()


def joined(a, b):
    return pl.pallas_call(
        join_kernel,
        out_shape=pltpu.VMEM((*a.shape[:2], 2 * a.shape[2]), a.dtype),
        in_specs=[ANY, ANY],
        out_specs=VMEM,
        scratch_shapes=[pltpu.SemaphoreType.DMA((2,))],
    )(a, b)


def lag_kernel(scale, offsets_ref, head_ref, both_ref, out_ref, x_ref, y_ref, xt_ref, diag_ref):
    shards, pair_tiles = both_ref.shape[:2]
    per = pair_tiles // 2
    tiles = shards * per
    rows = 2 * tiles

    def flat(ref, first, count):
        return ref.at[pl.ds(first, count)].reshape(2 * count, LANES)

    x_ref[0] = jnp.zeros((2, LANES), x_ref.dtype)
    flat(y_ref, tiles, tiles)[...] = jnp.zeros((rows, LANES), y_ref.dtype)

    def split(s, carry):
        flat(x_ref, 1 + s * per, per)[...] = flat(both_ref.at[s], 0, per)[...]
        flat(y_ref, s * per, per)[...] = flat(both_ref.at[s], per, per)[...]
        return carry

    lax.fori_loop(0, shards, split, 0, unroll=8)
    for part, first in ((0, 1), (1, 0)):
        xt_ref[pl.ds(part * LANES, LANES), :] = flat(x_ref, first, tiles)[...].T
    blocks = diag_ref.shape[0] // 8
    keep = lax.broadcasted_iota(jnp.int32, (LANES, LANES), 0) <= lax.broadcasted_iota(
        jnp.int32, (LANES, LANES), 1)
    xt = xt_ref[...]
    for k in range(0, blocks, 2):
        group = [j for j in (k, k + 1) if j < blocks]
        windows = [
            flat(y_ref, 0 if j == 0 else offsets_ref[j - 1], tiles)[...] for j in group
        ]
        window = jnp.concatenate(windows, axis=1) if len(windows) > 1 else windows[0]
        grid = jnp.dot(xt, window, preferred_element_type=jnp.float32)
        for n, j in enumerate(group):
            part = grid[:, n * LANES:(n + 1) * LANES]
            both = jnp.where(keep, part[:LANES], part[LANES:])
            acc = both[:8]
            for v in range(1, LANES // 8):
                acc = acc + pltpu.roll(both[8 * v:8 * v + 8], LANES - 8 * v, 1)
            diag_ref[pl.ds(8 * j, 8), :] = acc
    acc = diag_ref[...]
    sub = lax.broadcasted_iota(jnp.int32, acc.shape, 0)
    for bit in (1, 2, 4):
        acc = jnp.where((sub & bit) != 0, pltpu.roll(acc, LANES - bit, 1), acc)
    sums = jnp.sum(acc.reshape(blocks, 8, LANES), axis=1) * scale
    block = lax.broadcasted_iota(jnp.int32, sums.shape, 0)
    lag = lax.broadcasted_iota(jnp.int32, sums.shape, 1)
    sums = jnp.where((block > 0) | (lag < head_ref[0]), sums, jnp.zeros_like(sums))
    pieces, copies, width = out_ref.shape
    lane = lax.broadcasted_iota(jnp.int32, (copies, LANES), 1)
    for q in range(pieces):
        b, s = divmod(q * width, LANES)
        row = jnp.broadcast_to(sums[b:b + 1], (copies, LANES))
        if s:
            row = pltpu.roll(row, LANES - s, 1)
        if s + width > LANES:
            after = jnp.broadcast_to(sums[b + 1:b + 2], (copies, LANES))
            row = jnp.where(lane < LANES - s, row, pltpu.roll(after, LANES - s, 1))
        out_ref[q] = row[:, :width]


def lag_sums(both, offsets, head_len, scale, pieces, copies):
    shards, pair_tiles = both.shape[:2]
    tiles = shards * pair_tiles // 2
    blocks = offsets.shape[0] + 1
    return pl.pallas_call(
        functools.partial(lag_kernel, scale),
        out_shape=pltpu.VMEM((pieces, copies, blocks * LANES // pieces), jnp.float32),
        in_specs=[SMEM, SMEM, VMEM],
        out_specs=VMEM,
        scratch_shapes=[
            pltpu.VMEM((tiles + 1, 2, LANES), both.dtype),
            pltpu.VMEM((2 * tiles, 2, LANES), both.dtype),
            pltpu.VMEM((2 * LANES, 2 * tiles), both.dtype),
            pltpu.VMEM((8 * blocks, LANES), jnp.float32),
        ],
    )(offsets, head_len, pltpu.with_memory_space_constraint(both, pltpu.VMEM))


def local(saved_input, out_grad, block_offsets, head_len):
    filters, local_ch, tok_dev = saved_input.shape
    ctx_count, ch_count = lax.axis_size("ctx"), lax.axis_size("ch")
    scale = 1.0 / math.sqrt(tok_dev * ctx_count * local_ch * ch_count)
    both = joined(saved_input, out_grad)
    both = lax.all_to_all(both, "ctx", split_axis=0, concat_axis=0, tiled=True)
    tiles = both.shape[2] // LANES
    both = both.reshape(ctx_count, local_ch, tiles, LANES).transpose(0, 2, 1, 3)
    sums = lag_sums(both, block_offsets, head_len, scale, ctx_count, ch_count)
    sums = sums.reshape(ctx_count * ch_count, -1)
    got = lax.all_to_all(sums, ("ctx", "ch"), split_axis=0, concat_axis=0, tiled=True)
    return jnp.sum(got.reshape(filters, ch_count, -1), axis=1)


def solution(mesh):
    in_specs = (P(None, "ch", "ctx"), P(None, "ch", "ctx"), P(), P())
    return jax.shard_map(
        local, mesh=mesh, in_specs=in_specs, out_specs=P(None, "ctx"), check_vma=False
    )
```

```python
import functools
import math

import jax
import jax.numpy as jnp
from jax import lax
from jax.experimental import pallas as pl
from jax.experimental.pallas import tpu as pltpu
from jax.sharding import PartitionSpec as P

LANES = 128
VMEM = pl.BlockSpec(memory_space=pltpu.VMEM)
ANY = pl.BlockSpec(memory_space=pl.ANY)


def join_kernel(offsets_hbm, a_ref, b_ref, out_ref, order_ref, offsets_ref, sems):
    width = a_ref.shape[2]
    fetch = pltpu.make_async_copy(offsets_hbm, offsets_ref, sems.at[2])
    fetch.start()
    copies = [
        pltpu.make_async_copy(a_ref, out_ref.at[:, :, pl.ds(0, width)], sems.at[0]),
        pltpu.make_async_copy(b_ref, out_ref.at[:, :, pl.ds(width, width)], sems.at[1]),
    ]
    for c in copies:
        c.start()
    fetch.wait()
    blocks = offsets_ref.shape[0] + 1
    shape = (-(-blocks // 8) * 8, LANES)
    sub = lax.broadcasted_iota(jnp.int32, shape, 0)
    lane = lax.broadcasted_iota(jnp.int32, shape, 1)
    down = across = jnp.zeros(shape, jnp.int32)
    for k in range(1, blocks):
        down = jnp.where(sub == k, offsets_ref[k - 1], down)
        across = jnp.where(lane == k, offsets_ref[k - 1], across)
    below = (across < down) & (lane < blocks)
    rank = jnp.sum(below.astype(jnp.int32), axis=1, keepdims=True)
    here = (rank == lane) & (sub < blocks)
    order_ref[0:1] = jnp.sum(jnp.where(here, down, 0), axis=0, keepdims=True)
    order_ref[1:2] = jnp.sum(jnp.where(here, sub, 0), axis=0, keepdims=True)
    for c in copies:
        c.wait()


def joined(offsets, a, b):
    return pl.pallas_call(
        join_kernel,
        out_shape=(
            pltpu.VMEM((*a.shape[:2], 2 * a.shape[2]), a.dtype),
            pltpu.VMEM((8, LANES), jnp.int32),
        ),
        in_specs=[ANY, ANY, ANY],
        out_specs=(VMEM, VMEM),
        scratch_shapes=[
            pltpu.SMEM(offsets.shape, offsets.dtype),
            pltpu.SemaphoreType.DMA((3,)),
        ],
    )(offsets, a, b)


def lag_kernel(scale, order_vmem, both_ref, out_ref, order_ref, x_ref, y_ref, xt_ref, diag_ref, sem):
    fetch = pltpu.make_async_copy(order_vmem, order_ref, sem)
    fetch.start()
    shards, pair_tiles = both_ref.shape[:2]
    per = pair_tiles // 2
    tiles = shards * per
    rows = 2 * tiles

    def flat(ref, first, count):
        return ref.at[pl.ds(first, count)].reshape(2 * count, LANES)

    x_ref[0] = jnp.zeros((2, LANES), x_ref.dtype)
    flat(y_ref, tiles, y_ref.shape[0] - tiles)[...] = jnp.zeros(
        (2 * (y_ref.shape[0] - tiles), LANES), y_ref.dtype)

    def split(s, carry):
        flat(x_ref, 1 + s * per, per)[...] = flat(both_ref.at[s], 0, per)[...]
        flat(y_ref, s * per, per)[...] = flat(both_ref.at[s], per, per)[...]
        return carry

    lax.fori_loop(0, shards, split, 0, unroll=8)
    for part, first in ((0, 1), (1, 0)):
        xt_ref[pl.ds(part * LANES, LANES), :] = flat(x_ref, first, tiles)[...].T
    fetch.wait()
    blocks = diag_ref.shape[0] // 8
    chunks = tiles // LANES
    keep = lax.broadcasted_iota(jnp.int32, (LANES, LANES), 0) <= lax.broadcasted_iota(
        jnp.int32, (LANES, LANES), 1)

    def work(places, count):
        windows = [flat(y_ref, order_ref[0, p], count * LANES)[...] for p in places]
        window = jnp.concatenate(windows, axis=1) if len(windows) > 1 else windows[0]
        grid = jnp.dot(xt_ref[:, :2 * count * LANES], window, preferred_element_type=jnp.float32)
        for n, p in enumerate(places):
            part = grid[:, n * LANES:(n + 1) * LANES]
            both = jnp.where(keep, part[:LANES], part[LANES:])
            acc = both[:8]
            for v in range(1, LANES // 8):
                acc = acc + pltpu.roll(both[8 * v:8 * v + 8], LANES - 8 * v, 1)
            diag_ref[pl.ds(pl.multiple_of(8 * order_ref[1, p], 8), 8), :] = acc

    half = blocks // 4 * 2
    for p in range(0, half, 2):
        work((p, p + 1), chunks)
    needed = (tiles - order_ref[0, half] + LANES - 1) // LANES
    for count in range(1, chunks + 1):
        @pl.when(needed == count)
        def _(count=count):
            for p in range(half, blocks, 2):
                work(tuple(range(p, min(p + 2, blocks))), count)

    acc = diag_ref[...]
    sub = lax.broadcasted_iota(jnp.int32, acc.shape, 0)
    for bit in (1, 2, 4):
        acc = jnp.where((sub & bit) != 0, pltpu.roll(acc, LANES - bit, 1), acc)
    sums = jnp.sum(acc.reshape(blocks, 8, LANES), axis=1) * scale
    pieces, copies, width = out_ref.shape
    lane = lax.broadcasted_iota(jnp.int32, (copies, LANES), 1)
    for q in range(pieces):
        b, s = divmod(q * width, LANES)
        row = jnp.broadcast_to(sums[b:b + 1], (copies, LANES))
        if s:
            row = pltpu.roll(row, LANES - s, 1)
        if s + width > LANES:
            after = jnp.broadcast_to(sums[b + 1:b + 2], (copies, LANES))
            row = jnp.where(lane < LANES - s, row, pltpu.roll(after, LANES - s, 1))
        out_ref[q] = row[:, :width]


def lag_sums(both, order, blocks, scale, pieces, copies):
    shards, pair_tiles = both.shape[:2]
    tiles = shards * pair_tiles // 2
    return pl.pallas_call(
        functools.partial(lag_kernel, scale),
        out_shape=jax.ShapeDtypeStruct((pieces, copies, blocks * LANES // pieces), jnp.float32),
        in_specs=[VMEM, VMEM],
        out_specs=VMEM,
        scratch_shapes=[
            pltpu.SMEM(order.shape, order.dtype),
            pltpu.VMEM((tiles + 1, 2, LANES), both.dtype),
            pltpu.VMEM((2 * tiles + LANES, 2, LANES), both.dtype),
            pltpu.VMEM((2 * LANES, 2 * tiles), both.dtype),
            pltpu.VMEM((8 * blocks, LANES), jnp.float32),
            pltpu.SemaphoreType.DMA,
        ],
    )(*(pltpu.with_memory_space_constraint(a, pltpu.VMEM) for a in (order, both)))


def local(saved_input, out_grad, block_offsets, head_len):
    filters, local_ch, tok_dev = saved_input.shape
    ctx_count, ch_count = lax.axis_size("ctx"), lax.axis_size("ch")
    scale = 1.0 / math.sqrt(tok_dev * ctx_count * local_ch * ch_count)
    both, order = joined(block_offsets, saved_input, out_grad)
    both = lax.all_to_all(both, "ctx", split_axis=0, concat_axis=0, tiled=True)
    tiles = both.shape[2] // LANES
    both = both.reshape(ctx_count, local_ch, tiles, LANES).transpose(0, 2, 1, 3)
    blocks = block_offsets.shape[0] + 1
    sums = lag_sums(both, order, blocks, scale, ctx_count, ch_count)
    sums = sums.reshape(ctx_count * ch_count, -1)
    got = lax.all_to_all(sums, ("ctx", "ch"), split_axis=0, concat_axis=0, tiled=True)
    out = jnp.sum(got.reshape(filters, ch_count, -1), axis=1)
    lag = lax.broadcasted_iota(jnp.int32, out.shape, 1) + lax.axis_index("ctx") * out.shape[1]
    return jnp.where((lag >= LANES) | (lag < head_len[0]), out, jnp.zeros_like(out))


def solution(mesh):
    in_specs = (P(None, "ch", "ctx"), P(None, "ch", "ctx"), P(), P())
    return jax.shard_map(
        local, mesh=mesh, in_specs=in_specs, out_specs=P(None, "ctx"), check_vma=False
    )
```

```python
import functools
import math

import jax
import jax.numpy as jnp
from jax import lax
from jax.experimental import pallas as pl
from jax.experimental.pallas import tpu as pltpu
from jax.sharding import PartitionSpec as P

LANES = 128
VMEM = pl.BlockSpec(memory_space=pltpu.VMEM)
ANY = pl.BlockSpec(memory_space=pl.ANY)


def first_shard(shards):
    return 3 * shards // 4 + 1


def members(shards):
    return [(first_shard(shards) - i) % shards for i in range(shards)]


def join_kernel(offsets_hbm, a_ref, b_ref, out_ref, order_ref, offsets_ref, sems):
    width = a_ref.shape[2]
    fetch = pltpu.make_async_copy(offsets_hbm, offsets_ref, sems.at[2])
    fetch.start()
    copies = [
        pltpu.make_async_copy(a_ref, out_ref.at[:, :, pl.ds(0, width)], sems.at[0]),
        pltpu.make_async_copy(b_ref, out_ref.at[:, :, pl.ds(width, width)], sems.at[1]),
    ]
    for c in copies:
        c.start()
    fetch.wait()
    blocks = offsets_ref.shape[0] + 1
    shape = (-(-blocks // 8) * 8, LANES)
    sub = lax.broadcasted_iota(jnp.int32, shape, 0)
    lane = lax.broadcasted_iota(jnp.int32, shape, 1)
    down = across = jnp.zeros(shape, jnp.int32)
    for k in range(1, blocks):
        down = jnp.where(sub == k, offsets_ref[k - 1], down)
        across = jnp.where(lane == k, offsets_ref[k - 1], across)
    below = (across < down) & (lane < blocks)
    rank = jnp.sum(below.astype(jnp.int32), axis=1, keepdims=True)
    here = (rank == lane) & (sub < blocks)
    order_ref[0:1] = jnp.sum(jnp.where(here, down, 0), axis=0, keepdims=True)
    order_ref[1:2] = jnp.sum(jnp.where(here, sub, 0), axis=0, keepdims=True)
    for c in copies:
        c.wait()


def joined(offsets, a, b):
    return pl.pallas_call(
        join_kernel,
        out_shape=(
            pltpu.VMEM((*a.shape[:2], 2 * a.shape[2]), a.dtype),
            pltpu.VMEM((8, LANES), jnp.int32),
        ),
        in_specs=[ANY, ANY, ANY],
        out_specs=(VMEM, VMEM),
        scratch_shapes=[
            pltpu.SMEM(offsets.shape, offsets.dtype),
            pltpu.SemaphoreType.DMA((3,)),
        ],
    )(offsets, a, b)


def lag_kernel(scale, order_vmem, both_ref, out_ref, order_ref, x_ref, y_ref, xt_ref, diag_ref, sem):
    fetch = pltpu.make_async_copy(order_vmem, order_ref, sem)
    fetch.start()
    shards, pair_tiles = both_ref.shape[:2]
    per = pair_tiles // 2
    tiles = shards * per
    rows = 2 * tiles

    def flat(ref, first, count):
        return ref.at[pl.ds(first, count)].reshape(2 * count, LANES)

    x_ref[0] = jnp.zeros((2, LANES), x_ref.dtype)
    flat(y_ref, tiles, y_ref.shape[0] - tiles)[...] = jnp.zeros(
        (2 * (y_ref.shape[0] - tiles), LANES), y_ref.dtype)

    def split(s, carry):
        at = lax.rem(first_shard(shards) + shards - s, shards) * per
        flat(x_ref, 1 + at, per)[...] = flat(both_ref.at[s], 0, per)[...]
        flat(y_ref, at, per)[...] = flat(both_ref.at[s], per, per)[...]
        return carry

    lax.fori_loop(0, shards, split, 0, unroll=8)
    for part, first in ((0, 1), (1, 0)):
        xt_ref[pl.ds(part * LANES, LANES), :] = flat(x_ref, first, tiles)[...].T
    fetch.wait()
    blocks = diag_ref.shape[0] // 8
    chunks = tiles // LANES
    keep = lax.broadcasted_iota(jnp.int32, (LANES, LANES), 0) <= lax.broadcasted_iota(
        jnp.int32, (LANES, LANES), 1)

    def work(places, count):
        windows = [flat(y_ref, order_ref[0, p], count * LANES)[...] for p in places]
        window = jnp.concatenate(windows, axis=1) if len(windows) > 1 else windows[0]
        grid = jnp.dot(xt_ref[:, :2 * count * LANES], window, preferred_element_type=jnp.float32)
        for n, p in enumerate(places):
            part = grid[:, n * LANES:(n + 1) * LANES]
            both = jnp.where(keep, part[:LANES], part[LANES:])
            acc = both[:8]
            for v in range(1, LANES // 8):
                acc = acc + pltpu.roll(both[8 * v:8 * v + 8], LANES - 8 * v, 1)
            diag_ref[pl.ds(pl.multiple_of(8 * order_ref[1, p], 8), 8), :] = acc

    half = blocks // 4 * 2
    for p in range(0, half, 2):
        work((p, p + 1), chunks)
    needed = (tiles - order_ref[0, half] + LANES - 1) // LANES
    for count in range(1, chunks + 1):
        @pl.when(needed == count)
        def _(count=count):
            for p in range(half, blocks, 2):
                work(tuple(range(p, min(p + 2, blocks))), count)

    acc = diag_ref[...]
    sub = lax.broadcasted_iota(jnp.int32, acc.shape, 0)
    for bit in (1, 2, 4):
        acc = jnp.where((sub & bit) != 0, pltpu.roll(acc, LANES - bit, 1), acc)
    sums = jnp.sum(acc.reshape(blocks, 8, LANES), axis=1) * scale
    pieces, copies, width = out_ref.shape
    lane = lax.broadcasted_iota(jnp.int32, (copies, LANES), 1)
    for q, piece in enumerate(members(pieces)):
        b, s = divmod(piece * width, LANES)
        row = jnp.broadcast_to(sums[b:b + 1], (copies, LANES))
        if s:
            row = pltpu.roll(row, LANES - s, 1)
        if s + width > LANES:
            after = jnp.broadcast_to(sums[b + 1:b + 2], (copies, LANES))
            row = jnp.where(lane < LANES - s, row, pltpu.roll(after, LANES - s, 1))
        out_ref[q] = row[:, :width]


def lag_sums(both, order, blocks, scale, pieces, copies):
    shards, pair_tiles = both.shape[:2]
    tiles = shards * pair_tiles // 2
    return pl.pallas_call(
        functools.partial(lag_kernel, scale),
        out_shape=jax.ShapeDtypeStruct((pieces, copies, blocks * LANES // pieces), jnp.float32),
        in_specs=[VMEM, VMEM],
        out_specs=VMEM,
        scratch_shapes=[
            pltpu.SMEM(order.shape, order.dtype),
            pltpu.VMEM((tiles + 1, 2, LANES), both.dtype),
            pltpu.VMEM((2 * tiles + LANES, 2, LANES), both.dtype),
            pltpu.VMEM((2 * LANES, 2 * tiles), both.dtype),
            pltpu.VMEM((8 * blocks, LANES), jnp.float32),
            pltpu.SemaphoreType.DMA,
        ],
    )(*(pltpu.with_memory_space_constraint(a, pltpu.VMEM) for a in (order, both)))


def local(saved_input, out_grad, block_offsets, head_len):
    filters, local_ch, tok_dev = saved_input.shape
    ctx_count, ch_count = lax.axis_size("ctx"), lax.axis_size("ch")
    scale = 1.0 / math.sqrt(tok_dev * ctx_count * local_ch * ch_count)
    both, order = joined(block_offsets, saved_input, out_grad)
    both = lax.all_to_all(
        both, "ctx", split_axis=0, concat_axis=0, tiled=True,
        axis_index_groups=[members(ctx_count)])
    tiles = both.shape[2] // LANES
    both = both.reshape(ctx_count, local_ch, tiles, LANES).transpose(0, 2, 1, 3)
    blocks = block_offsets.shape[0] + 1
    pairs = ch_count // 2
    sums = lag_sums(both, order, blocks, scale, ctx_count, pairs)
    groups = [
        [c * ch_count + 2 * h + side for c in members(ctx_count) for h in (2, 3, 1, 0)]
        for side in range(2)
    ]
    got = lax.all_to_all(
        sums.reshape(ctx_count * pairs, -1), ("ctx", "ch"), split_axis=0, concat_axis=0, tiled=True,
        axis_index_groups=groups)
    out = jnp.sum(got.reshape(filters, pairs, -1), axis=1)
    out = out + lax.ppermute(out, "ch", [(h, h ^ 1) for h in range(ch_count)])
    lag = lax.broadcasted_iota(jnp.int32, out.shape, 1) + lax.axis_index("ctx") * out.shape[1]
    return jnp.where((lag >= LANES) | (lag < head_len[0]), out, jnp.zeros_like(out))


def solution(mesh):
    in_specs = (P(None, "ch", "ctx"), P(None, "ch", "ctx"), P(), P())
    return jax.shard_map(
        local, mesh=mesh, in_specs=in_specs, out_specs=P(None, "ctx"), check_vma=False
    )
```

```python
import functools
import math

import jax
import jax.numpy as jnp
from jax import lax
from jax.experimental import pallas as pl
from jax.experimental.pallas import tpu as pltpu
from jax.sharding import PartitionSpec as P

LANES = 128
VMEM = pl.BlockSpec(memory_space=pltpu.VMEM)
ANY = pl.BlockSpec(memory_space=pl.ANY)


def first_shard(shards):
    return 3 * shards // 4 + 1


def members(shards):
    return [(first_shard(shards) - i) % shards for i in range(shards)]


def join_kernel(offsets_hbm, a_ref, b_ref, out_ref, order_ref, offsets_ref, sems):
    width = a_ref.shape[2]
    fetch = pltpu.make_async_copy(offsets_hbm, offsets_ref, sems.at[2])
    fetch.start()
    copies = [
        pltpu.make_async_copy(a_ref, out_ref.at[:, :, pl.ds(0, width)], sems.at[0]),
        pltpu.make_async_copy(b_ref, out_ref.at[:, :, pl.ds(width, width)], sems.at[1]),
    ]
    for c in copies:
        c.start()
    fetch.wait()
    blocks = offsets_ref.shape[0] + 1
    shape = (-(-blocks // 8) * 8, LANES)
    sub = lax.broadcasted_iota(jnp.int32, shape, 0)
    lane = lax.broadcasted_iota(jnp.int32, shape, 1)
    down = across = jnp.zeros(shape, jnp.int32)
    for k in range(1, blocks):
        down = jnp.where(sub == k, offsets_ref[k - 1], down)
        across = jnp.where(lane == k, offsets_ref[k - 1], across)
    below = (across < down) & (lane < blocks)
    rank = jnp.sum(below.astype(jnp.int32), axis=1, keepdims=True)
    here = (rank == lane) & (sub < blocks)
    order_ref[0:1] = jnp.sum(jnp.where(here, down, 0), axis=0, keepdims=True)
    order_ref[1:2] = jnp.sum(jnp.where(here, sub, 0), axis=0, keepdims=True)
    for c in copies:
        c.wait()


def joined(offsets, a, b):
    return pl.pallas_call(
        join_kernel,
        out_shape=(
            pltpu.VMEM((*a.shape[:2], 2 * a.shape[2]), a.dtype),
            pltpu.VMEM((8, LANES), jnp.int32),
        ),
        in_specs=[ANY, ANY, ANY],
        out_specs=(VMEM, VMEM),
        scratch_shapes=[
            pltpu.SMEM(offsets.shape, offsets.dtype),
            pltpu.SemaphoreType.DMA((3,)),
        ],
    )(offsets, a, b)


def lag_kernel(scale, order_vmem, both_ref, out_ref, order_ref, x_ref, y_ref, xt_ref, diag_ref, sem):
    fetch = pltpu.make_async_copy(order_vmem, order_ref, sem)
    fetch.start()
    shards, pair_tiles = both_ref.shape[:2]
    per = pair_tiles // 2
    tiles = shards * per
    rows = 2 * tiles

    def flat(ref, first, count):
        return ref.at[pl.ds(first, count)].reshape(2 * count, LANES)

    x_ref[0] = jnp.zeros((2, LANES), x_ref.dtype)
    flat(y_ref, tiles, y_ref.shape[0] - tiles)[...] = jnp.zeros(
        (2 * (y_ref.shape[0] - tiles), LANES), y_ref.dtype)

    def split(s, carry):
        at = lax.rem(first_shard(shards) + shards - s, shards) * per
        flat(x_ref, 1 + at, per)[...] = flat(both_ref.at[s], 0, per)[...]
        flat(y_ref, at, per)[...] = flat(both_ref.at[s], per, per)[...]
        return carry

    lax.fori_loop(0, shards, split, 0, unroll=8)
    for part, first in ((0, 1), (1, 0)):
        xt_ref[pl.ds(part * LANES, LANES), :] = flat(x_ref, first, tiles)[...].T
    fetch.wait()
    blocks = diag_ref.shape[0] // 8
    chunks = tiles // LANES
    keep = lax.broadcasted_iota(jnp.int32, (LANES, LANES), 0) <= lax.broadcasted_iota(
        jnp.int32, (LANES, LANES), 1)

    def work(places, count):
        windows = [flat(y_ref, order_ref[0, p], count * LANES)[...] for p in places]
        window = jnp.concatenate(windows, axis=1) if len(windows) > 1 else windows[0]
        grid = jnp.dot(xt_ref[:, :2 * count * LANES], window, preferred_element_type=jnp.float32)
        for n, p in enumerate(places):
            part = grid[:, n * LANES:(n + 1) * LANES]
            both = jnp.where(keep, part[:LANES], part[LANES:])
            acc = both[:8]
            for v in range(1, LANES // 8):
                acc = acc + pltpu.roll(both[8 * v:8 * v + 8], LANES - 8 * v, 1)
            diag_ref[pl.ds(pl.multiple_of(8 * order_ref[1, p], 8), 8), :] = acc

    half = blocks // 4 * 2
    for p in range(0, half, 2):
        work((p, p + 1), chunks)
    needed = (tiles - order_ref[0, half] + LANES - 1) // LANES
    for count in range(1, chunks + 1):
        @pl.when(needed == count)
        def _(count=count):
            for p in range(half, blocks, 2):
                work(tuple(range(p, min(p + 2, blocks))), count)

    acc = diag_ref[...]
    sub = lax.broadcasted_iota(jnp.int32, acc.shape, 0)
    for bit in (1, 2, 4):
        acc = jnp.where((sub & bit) != 0, pltpu.roll(acc, LANES - bit, 1), acc)
    sums = jnp.sum(acc.reshape(blocks, 8, LANES), axis=1) * scale
    pieces, copies, width = out_ref.shape
    lane = lax.broadcasted_iota(jnp.int32, (copies, LANES), 1)
    for q, piece in enumerate(members(pieces)):
        b, s = divmod(piece * width, LANES)
        row = jnp.broadcast_to(sums[b:b + 1], (copies, LANES))
        if s:
            row = pltpu.roll(row, LANES - s, 1)
        if s + width > LANES:
            after = jnp.broadcast_to(sums[b + 1:b + 2], (copies, LANES))
            row = jnp.where(lane < LANES - s, row, pltpu.roll(after, LANES - s, 1))
        out_ref[q] = row[:, :width]


def lag_sums(both, order, blocks, scale, pieces, copies):
    shards, pair_tiles = both.shape[:2]
    tiles = shards * pair_tiles // 2
    return pl.pallas_call(
        functools.partial(lag_kernel, scale),
        out_shape=pltpu.VMEM((pieces, copies, blocks * LANES // pieces), jnp.float32),
        in_specs=[VMEM, VMEM],
        out_specs=VMEM,
        scratch_shapes=[
            pltpu.SMEM(order.shape, order.dtype),
            pltpu.VMEM((tiles + 1, 2, LANES), both.dtype),
            pltpu.VMEM((2 * tiles + LANES, 2, LANES), both.dtype),
            pltpu.VMEM((2 * LANES, 2 * tiles), both.dtype),
            pltpu.VMEM((8 * blocks, LANES), jnp.float32),
            pltpu.SemaphoreType.DMA,
        ],
    )(*(pltpu.with_memory_space_constraint(a, pltpu.VMEM) for a in (order, both)))


def finish_kernel(head_ref, a_ref, b_ref, out_ref):
    total = a_ref[...] + b_ref[...]
    lag = lax.broadcasted_iota(jnp.int32, total.shape, 1) + lax.axis_index("ctx") * total.shape[1]
    out_ref[...] = jnp.where((lag >= LANES) | (lag < head_ref[0]), total, jnp.zeros_like(total))


def finished(head_len, a, b):
    return pl.pallas_call(
        finish_kernel,
        out_shape=jax.ShapeDtypeStruct(a.shape, a.dtype),
        in_specs=[pl.BlockSpec(memory_space=pltpu.SMEM), VMEM, VMEM],
        out_specs=VMEM,
    )(head_len, *(pltpu.with_memory_space_constraint(p, pltpu.VMEM) for p in (a, b)))


def local(saved_input, out_grad, block_offsets, head_len):
    filters, local_ch, tok_dev = saved_input.shape
    ctx_count, ch_count = lax.axis_size("ctx"), lax.axis_size("ch")
    scale = 1.0 / math.sqrt(tok_dev * ctx_count * local_ch * ch_count)
    both, order = joined(block_offsets, saved_input, out_grad)
    both = lax.all_to_all(
        both, "ctx", split_axis=0, concat_axis=0, tiled=True,
        axis_index_groups=[members(ctx_count)])
    tiles = both.shape[2] // LANES
    both = both.reshape(ctx_count, local_ch, tiles, LANES).transpose(0, 2, 1, 3)
    blocks = block_offsets.shape[0] + 1
    pairs = ch_count // 2
    sums = lag_sums(both, order, blocks, scale, ctx_count, pairs)
    groups = [
        [c * ch_count + 2 * h + side for c in members(ctx_count) for h in (2, 3, 1, 0)]
        for side in range(2)
    ]
    got = lax.all_to_all(
        sums.reshape(ctx_count * pairs, -1), ("ctx", "ch"), split_axis=0, concat_axis=0, tiled=True,
        axis_index_groups=groups)
    out = jnp.sum(got.reshape(filters, pairs, -1), axis=1)
    out, head_len = lax.optimization_barrier((out, head_len))
    twin = lax.ppermute(out, "ch", [(h, h ^ 1) for h in range(ch_count)])
    return finished(head_len, out, twin)


def solution(mesh):
    in_specs = (P(None, "ch", "ctx"), P(None, "ch", "ctx"), P(), P())
    return jax.shard_map(
        local, mesh=mesh, in_specs=in_specs, out_specs=P(None, "ctx"), check_vma=False
    )
```

```python
import functools
import math

import jax
import jax.numpy as jnp
from jax import lax
from jax.experimental import pallas as pl
from jax.experimental.pallas import tpu as pltpu
from jax.sharding import PartitionSpec as P

LANES = 128
VMEM = pl.BlockSpec(memory_space=pltpu.VMEM)
ANY = pl.BlockSpec(memory_space=pl.ANY)


def first_shard(shards):
    return 3 * shards // 4 + 1


def members(shards):
    return [(first_shard(shards) - i) % shards for i in range(shards)]


def join_kernel(offsets_hbm, a_ref, b_ref, out_ref, order_ref, offsets_ref, sems):
    width = a_ref.shape[2]
    fetch = pltpu.make_async_copy(offsets_hbm, offsets_ref, sems.at[2])
    fetch.start()
    copies = [
        pltpu.make_async_copy(a_ref, out_ref.at[:, :, pl.ds(0, width)], sems.at[0]),
        pltpu.make_async_copy(b_ref, out_ref.at[:, :, pl.ds(width, width)], sems.at[1]),
    ]
    for c in copies:
        c.start()
    fetch.wait()
    blocks = offsets_ref.shape[0] + 1
    shape = (-(-blocks // 8) * 8, LANES)
    sub = lax.broadcasted_iota(jnp.int32, shape, 0)
    lane = lax.broadcasted_iota(jnp.int32, shape, 1)
    down = across = jnp.zeros(shape, jnp.int32)
    for k in range(1, blocks):
        down = jnp.where(sub == k, offsets_ref[k - 1], down)
        across = jnp.where(lane == k, offsets_ref[k - 1], across)
    below = (across < down) & (lane < blocks)
    rank = jnp.sum(below.astype(jnp.int32), axis=1, keepdims=True)
    here = (rank == lane) & (sub < blocks)
    order_ref[0:1] = jnp.sum(jnp.where(here, down, 0), axis=0, keepdims=True)
    order_ref[1:2] = jnp.sum(jnp.where(here, sub, 0), axis=0, keepdims=True)
    for c in copies:
        c.wait()


def joined(offsets, a, b):
    return pl.pallas_call(
        join_kernel,
        out_shape=(
            pltpu.VMEM((*a.shape[:2], 2 * a.shape[2]), a.dtype),
            pltpu.VMEM((8, LANES), jnp.int32),
        ),
        in_specs=[ANY, ANY, ANY],
        out_specs=(VMEM, VMEM),
        scratch_shapes=[
            pltpu.SMEM(offsets.shape, offsets.dtype),
            pltpu.SemaphoreType.DMA((3,)),
        ],
    )(offsets, a, b)


def lag_kernel(scale, order_vmem, both_ref, out_ref, order_ref, x_ref, y_ref, xt_ref, diag_ref, sem):
    fetch = pltpu.make_async_copy(order_vmem, order_ref, sem)
    fetch.start()
    shards, pair_tiles = both_ref.shape[:2]
    per = pair_tiles // 2
    tiles = shards * per
    rows = 2 * tiles

    def flat(ref, first, count):
        return ref.at[pl.ds(first, count)].reshape(2 * count, LANES)

    x_ref[0] = jnp.zeros((2, LANES), x_ref.dtype)
    flat(y_ref, tiles, y_ref.shape[0] - tiles)[...] = jnp.zeros(
        (2 * (y_ref.shape[0] - tiles), LANES), y_ref.dtype)

    def split(s, carry):
        at = lax.rem(first_shard(shards) + shards - s, shards) * per
        flat(x_ref, 1 + at, per)[...] = flat(both_ref.at[s], 0, per)[...]
        flat(y_ref, at, per)[...] = flat(both_ref.at[s], per, per)[...]
        return carry

    lax.fori_loop(0, shards, split, 0, unroll=8)
    for part, first in ((0, 1), (1, 0)):
        xt_ref[pl.ds(part * LANES, LANES), :] = flat(x_ref, first, tiles)[...].T
    fetch.wait()
    blocks = diag_ref.shape[0] // 8
    chunks = tiles // LANES
    keep = lax.broadcasted_iota(jnp.int32, (LANES, LANES), 0) <= lax.broadcasted_iota(
        jnp.int32, (LANES, LANES), 1)

    def work(places, count):
        windows = [flat(y_ref, order_ref[0, p], count * LANES)[...] for p in places]
        window = jnp.concatenate(windows, axis=1) if len(windows) > 1 else windows[0]
        grid = jnp.dot(xt_ref[:, :2 * count * LANES], window, preferred_element_type=jnp.float32)
        for n, p in enumerate(places):
            part = grid[:, n * LANES:(n + 1) * LANES]
            both = jnp.where(keep, part[:LANES], part[LANES:])
            acc = both[:8]
            for v in range(1, LANES // 8):
                acc = acc + pltpu.roll(both[8 * v:8 * v + 8], LANES - 8 * v, 1)
            diag_ref[pl.ds(pl.multiple_of(8 * order_ref[1, p], 8), 8), :] = acc

    half = blocks // 4 * 2
    for p in range(0, half, 2):
        work((p, p + 1), chunks)
    needed = (tiles - order_ref[0, half] + LANES - 1) // LANES
    for count in range(1, chunks + 1):
        @pl.when(needed == count)
        def _(count=count):
            for p in range(half, blocks, 2):
                work(tuple(range(p, min(p + 2, blocks))), count)

    acc = diag_ref[...]
    sub = lax.broadcasted_iota(jnp.int32, acc.shape, 0)
    for bit in (1, 2, 4):
        acc = jnp.where((sub & bit) != 0, pltpu.roll(acc, LANES - bit, 1), acc)
    sums = jnp.sum(acc.reshape(blocks, 8, LANES), axis=1) * scale
    pieces, copies, width = out_ref.shape
    lane = lax.broadcasted_iota(jnp.int32, (copies, LANES), 1)
    for q, piece in enumerate(members(pieces)):
        b, s = divmod(piece * width, LANES)
        row = jnp.broadcast_to(sums[b:b + 1], (copies, LANES))
        if s:
            row = pltpu.roll(row, LANES - s, 1)
        if s + width > LANES:
            after = jnp.broadcast_to(sums[b + 1:b + 2], (copies, LANES))
            row = jnp.where(lane < LANES - s, row, pltpu.roll(after, LANES - s, 1))
        out_ref[q] = row[:, :width]


def lag_sums(both, order, blocks, scale, pieces, copies):
    shards, pair_tiles = both.shape[:2]
    tiles = shards * pair_tiles // 2
    return pl.pallas_call(
        functools.partial(lag_kernel, scale),
        out_shape=pltpu.VMEM((pieces, copies, blocks * LANES // pieces), jnp.float32),
        in_specs=[VMEM, VMEM],
        out_specs=VMEM,
        scratch_shapes=[
            pltpu.SMEM(order.shape, order.dtype),
            pltpu.VMEM((tiles + 1, 2, LANES), both.dtype),
            pltpu.VMEM((2 * tiles + LANES, 2, LANES), both.dtype),
            pltpu.VMEM((2 * LANES, 2 * tiles), both.dtype),
            pltpu.VMEM((8 * blocks, LANES), jnp.float32),
            pltpu.SemaphoreType.DMA,
        ],
    )(*(pltpu.with_memory_space_constraint(a, pltpu.VMEM) for a in (order, both)))


def finish_kernel(head_ref, a_ref, b_ref, out_ref):
    total = a_ref[...] + b_ref[...]
    lag = lax.broadcasted_iota(jnp.int32, total.shape, 1) + lax.axis_index("ctx") * total.shape[1]
    out_ref[...] = jnp.where((lag >= LANES) | (lag < head_ref[0]), total, jnp.zeros_like(total))


def finished(head_len, a, b):
    return pl.pallas_call(
        finish_kernel,
        out_shape=jax.ShapeDtypeStruct(a.shape, a.dtype),
        in_specs=[pl.BlockSpec(memory_space=pltpu.SMEM), VMEM, VMEM],
        out_specs=VMEM,
    )(head_len, *(pltpu.with_memory_space_constraint(p, pltpu.VMEM) for p in (a, b)))


def local(saved_input, out_grad, block_offsets, head_len):
    filters, local_ch, tok_dev = saved_input.shape
    ctx_count, ch_count = lax.axis_size("ctx"), lax.axis_size("ch")
    scale = 1.0 / math.sqrt(tok_dev * ctx_count * local_ch * ch_count)
    both, order = joined(block_offsets, saved_input, out_grad)
    both = lax.all_to_all(
        both, "ctx", split_axis=0, concat_axis=0, tiled=True,
        axis_index_groups=[members(ctx_count)])
    tiles = both.shape[2] // LANES
    both = both.reshape(ctx_count, local_ch, tiles, LANES).transpose(0, 2, 1, 3)
    blocks = block_offsets.shape[0] + 1
    pairs = ch_count // 2
    sums = lag_sums(both, order, blocks, scale, ctx_count, pairs)
    halves = [(h + pairs // 2) % pairs for h in range(pairs)], range(pairs, ch_count)
    groups = [[c * ch_count + h for c in members(ctx_count) for h in half] for half in halves]
    got = lax.all_to_all(
        sums.reshape(ctx_count * pairs, -1), ("ctx", "ch"), split_axis=0, concat_axis=0, tiled=True,
        axis_index_groups=groups)
    out = jnp.sum(got.reshape(filters, pairs, -1), axis=1)
    out, head_len = lax.optimization_barrier((out, head_len))
    twin = lax.ppermute(out, "ch", [(h, (ch_count - 1 - h) ^ 1) for h in range(ch_count)])
    return finished(head_len, out, twin)


def solution(mesh):
    in_specs = (P(None, "ch", "ctx"), P(None, "ch", "ctx"), P(), P())
    return jax.shard_map(
        local, mesh=mesh, in_specs=in_specs, out_specs=P(None, "ctx"), check_vma=False
    )
```

```python
import functools
import math

import jax
import jax.numpy as jnp
from jax import lax
from jax.experimental import pallas as pl
from jax.experimental.pallas import tpu as pltpu
from jax.sharding import PartitionSpec as P

LANES = 128
VMEM = pl.BlockSpec(memory_space=pltpu.VMEM)
ANY = pl.BlockSpec(memory_space=pl.ANY)


def first_shard(shards):
    return 3 * shards // 4 + 3


def members(shards):
    return [(first_shard(shards) - i) % shards for i in range(shards)]


def join_kernel(offsets_hbm, a_ref, b_ref, out_ref, order_ref, offsets_ref, sems):
    width = a_ref.shape[2]
    fetch = pltpu.make_async_copy(offsets_hbm, offsets_ref, sems.at[2])
    fetch.start()
    copies = [
        pltpu.make_async_copy(a_ref, out_ref.at[:, :, pl.ds(0, width)], sems.at[0]),
        pltpu.make_async_copy(b_ref, out_ref.at[:, :, pl.ds(width, width)], sems.at[1]),
    ]
    for c in copies:
        c.start()
    fetch.wait()
    blocks = offsets_ref.shape[0] + 1
    shape = (-(-blocks // 8) * 8, LANES)
    sub = lax.broadcasted_iota(jnp.int32, shape, 0)
    lane = lax.broadcasted_iota(jnp.int32, shape, 1)
    down = across = jnp.zeros(shape, jnp.int32)
    for k in range(1, blocks):
        down = jnp.where(sub == k, offsets_ref[k - 1], down)
        across = jnp.where(lane == k, offsets_ref[k - 1], across)
    below = (across < down) & (lane < blocks)
    rank = jnp.sum(below.astype(jnp.int32), axis=1, keepdims=True)
    here = (rank == lane) & (sub < blocks)
    order_ref[0:1] = jnp.sum(jnp.where(here, down, 0), axis=0, keepdims=True)
    order_ref[1:2] = jnp.sum(jnp.where(here, sub, 0), axis=0, keepdims=True)
    for c in copies:
        c.wait()


def joined(offsets, a, b):
    return pl.pallas_call(
        join_kernel,
        out_shape=(
            pltpu.VMEM((*a.shape[:2], 2 * a.shape[2]), a.dtype),
            pltpu.VMEM((8, LANES), jnp.int32),
        ),
        in_specs=[ANY, ANY, ANY],
        out_specs=(VMEM, VMEM),
        scratch_shapes=[
            pltpu.SMEM(offsets.shape, offsets.dtype),
            pltpu.SemaphoreType.DMA((3,)),
        ],
    )(offsets, a, b)


def lag_kernel(scale, order_vmem, both_ref, out_ref, order_ref, x_ref, y_ref, xt_ref, diag_ref, sem):
    fetch = pltpu.make_async_copy(order_vmem, order_ref, sem)
    fetch.start()
    shards, pair_tiles = both_ref.shape[:2]
    per = pair_tiles // 2
    tiles = shards * per
    rows = 2 * tiles

    def flat(ref, first, count):
        return ref.at[pl.ds(first, count)].reshape(2 * count, LANES)

    x_ref[0] = jnp.zeros((2, LANES), x_ref.dtype)
    flat(y_ref, tiles, y_ref.shape[0] - tiles)[...] = jnp.zeros(
        (2 * (y_ref.shape[0] - tiles), LANES), y_ref.dtype)

    def split(s, carry):
        at = lax.rem(first_shard(shards) + shards - s, shards) * per
        flat(x_ref, 1 + at, per)[...] = flat(both_ref.at[s], 0, per)[...]
        flat(y_ref, at, per)[...] = flat(both_ref.at[s], per, per)[...]
        return carry

    lax.fori_loop(0, shards, split, 0, unroll=8)
    for part, first in ((0, 1), (1, 0)):
        xt_ref[pl.ds(part * LANES, LANES), :] = flat(x_ref, first, tiles)[...].T
    fetch.wait()
    blocks = diag_ref.shape[0] // 8
    chunks = tiles // LANES
    keep = lax.broadcasted_iota(jnp.int32, (LANES, LANES), 0) <= lax.broadcasted_iota(
        jnp.int32, (LANES, LANES), 1)

    def work(places, count):
        windows = [flat(y_ref, order_ref[0, p], count * LANES)[...] for p in places]
        window = jnp.concatenate(windows, axis=1) if len(windows) > 1 else windows[0]
        grid = jnp.dot(xt_ref[:, :2 * count * LANES], window, preferred_element_type=jnp.float32)
        for n, p in enumerate(places):
            part = grid[:, n * LANES:(n + 1) * LANES]
            both = jnp.where(keep, part[:LANES], part[LANES:])
            acc = both[:8]
            for v in range(1, LANES // 8):
                acc = acc + pltpu.roll(both[8 * v:8 * v + 8], LANES - 8 * v, 1)
            diag_ref[pl.ds(pl.multiple_of(8 * order_ref[1, p], 8), 8), :] = acc

    half = blocks // 4 * 2
    for p in range(0, half, 2):
        work((p, p + 1), chunks)
    needed = (tiles - order_ref[0, half] + LANES - 1) // LANES
    for count in range(1, chunks + 1):
        @pl.when(needed == count)
        def _(count=count):
            for p in range(half, blocks, 2):
                work(tuple(range(p, min(p + 2, blocks))), count)

    acc = diag_ref[...]
    sub = lax.broadcasted_iota(jnp.int32, acc.shape, 0)
    for bit in (1, 2, 4):
        acc = jnp.where((sub & bit) != 0, pltpu.roll(acc, LANES - bit, 1), acc)
    sums = jnp.sum(acc.reshape(blocks, 8, LANES), axis=1) * scale
    pieces, copies, width = out_ref.shape
    lane = lax.broadcasted_iota(jnp.int32, (copies, LANES), 1)
    for q, piece in enumerate(members(pieces)):
        b, s = divmod(piece * width, LANES)
        row = jnp.broadcast_to(sums[b:b + 1], (copies, LANES))
        if s:
            row = pltpu.roll(row, LANES - s, 1)
        if s + width > LANES:
            after = jnp.broadcast_to(sums[b + 1:b + 2], (copies, LANES))
            row = jnp.where(lane < LANES - s, row, pltpu.roll(after, LANES - s, 1))
        out_ref[q] = row[:, :width]


def lag_sums(both, order, blocks, scale, pieces, copies):
    shards, pair_tiles = both.shape[:2]
    tiles = shards * pair_tiles // 2
    return pl.pallas_call(
        functools.partial(lag_kernel, scale),
        out_shape=pltpu.VMEM((pieces, copies, blocks * LANES // pieces), jnp.float32),
        in_specs=[VMEM, VMEM],
        out_specs=VMEM,
        scratch_shapes=[
            pltpu.SMEM(order.shape, order.dtype),
            pltpu.VMEM((tiles + 1, 2, LANES), both.dtype),
            pltpu.VMEM((2 * tiles + LANES, 2, LANES), both.dtype),
            pltpu.VMEM((2 * LANES, 2 * tiles), both.dtype),
            pltpu.VMEM((8 * blocks, LANES), jnp.float32),
            pltpu.SemaphoreType.DMA,
        ],
    )(*(pltpu.with_memory_space_constraint(a, pltpu.VMEM) for a in (order, both)))


def finish_kernel(head_ref, a_ref, b_ref, out_ref):
    total = a_ref[...] + b_ref[...]
    lag = lax.broadcasted_iota(jnp.int32, total.shape, 1) + lax.axis_index("ctx") * total.shape[1]
    out_ref[...] = jnp.where((lag >= LANES) | (lag < head_ref[0]), total, jnp.zeros_like(total))


def finished(head_len, a, b):
    return pl.pallas_call(
        finish_kernel,
        out_shape=jax.ShapeDtypeStruct(a.shape, a.dtype),
        in_specs=[pl.BlockSpec(memory_space=pltpu.SMEM), VMEM, VMEM],
        out_specs=VMEM,
    )(head_len, *(pltpu.with_memory_space_constraint(p, pltpu.VMEM) for p in (a, b)))


def local(saved_input, out_grad, block_offsets, head_len):
    filters, local_ch, tok_dev = saved_input.shape
    ctx_count, ch_count = lax.axis_size("ctx"), lax.axis_size("ch")
    scale = 1.0 / math.sqrt(tok_dev * ctx_count * local_ch * ch_count)
    both, order = joined(block_offsets, saved_input, out_grad)
    both = lax.all_to_all(
        both, "ctx", split_axis=0, concat_axis=0, tiled=True,
        axis_index_groups=[members(ctx_count)])
    tiles = both.shape[2] // LANES
    both = both.reshape(ctx_count, local_ch, tiles, LANES).transpose(0, 2, 1, 3)
    blocks = block_offsets.shape[0] + 1
    pairs = ch_count // 2
    sums = lag_sums(both, order, blocks, scale, ctx_count, pairs)
    halves = [(h + pairs // 2) % pairs for h in range(pairs)], range(pairs, ch_count)
    groups = [[c * ch_count + h for c in members(ctx_count) for h in half] for half in halves]
    got = lax.all_to_all(
        sums.reshape(ctx_count * pairs, -1), ("ctx", "ch"), split_axis=0, concat_axis=0, tiled=True,
        axis_index_groups=groups)
    out = jnp.sum(got.reshape(filters, pairs, -1), axis=1)
    out, head_len = lax.optimization_barrier((out, head_len))
    twin = lax.ppermute(out, "ch", [(h, (ch_count - 1 - h) ^ 1) for h in range(ch_count)])
    return finished(head_len, out, twin)


def solution(mesh):
    in_specs = (P(None, "ch", "ctx"), P(None, "ch", "ctx"), P(), P())
    return jax.shard_map(
        local, mesh=mesh, in_specs=in_specs, out_specs=P(None, "ctx"), check_vma=False
    )
```
